256 devices in a mesh: cuts: 8 (over x_lo, y), gz: 32 (over z, x_hi, core).
Axes of the slice: x: 4 (x_hi: 2, x_lo: 2; x = x_hi * 2 + x_lo), y: 4, z: 8, core: 2. Of those that a mesh axis runs over, the one named last changes fastest.
Arguments:
- vectors: float32 [8, 32, 64, 128, 128], P('cuts', None, 'gz'), may hold values from -9 to 9
- onsite: float32 [64, 128, 128], P('gz'), may hold values from -8.25 to 8.25
- center: float32 [8], P('cuts'), may hold values from -3 to 3
- inv_half: float32 [8], P('cuts'), may hold values from 0.06 to 0.1
- cheb_coef: float32 [8, 3], P('cuts'), may hold values from 0.5 to 1.5
Outputs:
- basis: float32 [8, 64, 64, 128, 128], P('cuts', None, 'gz')
- projected: float32 [8, 64, 64], P('cuts')
The draws below stay inside these ranges and needn't reach their ends.
All inputs are finite; a program needn't handle non-finite values.
Results may differ from the reference program's by a relative error of at most 0.00018.
Values sent between devices are 32-bit elements; how exact they have to be, the bound alone decides.
A program may use at most 128 MiB of HBM per device.

```python
import jax
import jax.numpy as jnp
from jax import lax

K = 32
LX = 128
LY = 128
NZ = 64
N_CUTS = 8


def draw_vectors(key, part):
    key_shared = jax.random.fold_in(key, 11)
    key_own = jax.random.fold_in(key, 12)
    key_common = jax.random.fold_in(key, 13)
    shared = jnp.clip(jax.random.normal(key_shared, (1, K, NZ, LX, LY), jnp.float32), -6.0, 6.0)
    own = jnp.clip(jax.random.normal(key_own, (N_CUTS, K, NZ, LX, LY), jnp.float32), -6.0, 6.0)
    common = jnp.clip(jax.random.normal(key_common, (1, 1, NZ, LX, LY), jnp.float32), -6.0, 6.0)
    return 0.6 * shared + 0.5 * own + 0.4 * common


def levels(stream_key, extent, cuts, low, top_value):
    factor_of = 1.0
    for axis_at, parts in cuts:
        heights = jax.random.uniform(jax.random.fold_in(jax.random.fold_in(stream_key, 6), axis_at), (parts,), jnp.float32, low / len(cuts), top_value / len(cuts))
        factor_of = factor_of * jnp.repeat(jnp.exp(heights), extent[axis_at] // parts).reshape((-1,) + (1,) * (len(extent) - 1 - axis_at))
    return factor_of


def setup_inputs(seed: int = 0) -> dict:
    splits = jax.random.split(jax.random.key(seed), 6)
    return {
        "vectors": draw_vectors(jax.random.fold_in(splits[5], 71), 0),
        "onsite": jnp.clip(jax.random.uniform(splits[1], (NZ, LX, LY), jnp.float32, -8.25, 8.25) * levels(splits[1], (NZ, LX, LY), ((0, 32),), -0.4, 0.0), -8.25, 8.25),
        "center": jnp.clip(jax.random.uniform(splits[2], (N_CUTS,), jnp.float32, -3.0, 3.0) * levels(splits[2], (N_CUTS,), ((0, 8),), -0.4, 0.0), -3.0, 3.0),
        "inv_half": jnp.clip(0.06 + 0.040000003 * jax.random.uniform(splits[3], (N_CUTS,), jnp.float32) ** levels(splits[3], (N_CUTS,), ((0, 8),), -0.2, 0.2), 0.06, 0.1),
        "cheb_coef": jnp.clip(0.5 + 1.0 * jax.random.uniform(splits[4], (N_CUTS, 3), jnp.float32) ** levels(splits[4], (N_CUTS, 3), ((0, 8),), -0.2, 0.2), 0.5, 1.5),
    }


def neighbours_xy(middle):
    padded = jnp.pad(middle, ((0, 0), (0, 0), (1, 1), (1, 1)))
    return padded[:, :, 2:, 1:-1] + padded[:, :, :-2, 1:-1] + padded[:, :, 1:-1, 2:] + padded[:, :, 1:-1, :-2]

def hamiltonian(field, onsite):
    along_z = jnp.roll(field, 1, axis=1) + jnp.roll(field, -1, axis=1)
    return onsite[None] * field - along_z - neighbours_xy(field)

def reference(vectors, onsite, center, inv_half, cheb_coef):
    sites_all = NZ * LX * LY
    identity = jnp.eye(2 * K, dtype=jnp.float32)
    filtered = []
    for cut_index in range(N_CUTS):
        start = vectors[cut_index]
        first = inv_half[cut_index] * (hamiltonian(start, onsite) - center[cut_index] * start)
        second = 2.0 * inv_half[cut_index] * (hamiltonian(first, onsite) - center[cut_index] * first) - start
        filtered.append(cheb_coef[cut_index, 0] * start + cheb_coef[cut_index, 1] * first + cheb_coef[cut_index, 2] * second)
    bases = []
    projections = []
    for cut_index in range(N_CUTS):
        if cut_index + 1 < N_CUTS:
            partner = filtered[cut_index + 1]
        else:
            partner = jnp.zeros_like(filtered[cut_index])
        union = jnp.concatenate([filtered[cut_index], partner], 0).reshape(2 * K, -1)
        gram = jnp.dot(union.astype(jnp.float32), union.T.astype(jnp.float32), precision=lax.Precision.HIGHEST, preferred_element_type=jnp.float32) / sites_all + 0.25 * identity
        factor = jnp.linalg.cholesky(gram)
        inverse = jax.scipy.linalg.solve_triangular(factor, identity, lower=True)
        basis = jnp.dot(inverse.astype(jnp.float32), union.astype(jnp.float32), precision=lax.Precision.HIGHEST, preferred_element_type=jnp.float32)
        images = hamiltonian(basis.reshape(2 * K, NZ, LX, LY), onsite).reshape(2 * K, -1)
        projections.append(jnp.dot(basis.astype(jnp.float32), images.T.astype(jnp.float32), precision=lax.Precision.HIGHEST, preferred_element_type=jnp.float32) / sites_all)
        bases.append(basis.reshape(2 * K, NZ, LX, LY))
    return (jnp.stack(bases), jnp.stack(projections))
```

```python
import functools

import jax
import jax.numpy as jnp
from jax import lax
from jax.experimental import pallas as pl
from jax.experimental.pallas import tpu as pltpu
from jax.sharding import PartitionSpec as P

MESH = pl.DeviceIdType.MESH
K = 32
LX = 128
LY = 128
XR = 8
NC = LX // XR
LAG = 2
N_CUTS = 8
N_GZ = 32
SITES = 64 * 128 * 128
F32 = jnp.float32
BF16 = jnp.bfloat16


def lanes(v):
    at = lax.broadcasted_iota(jnp.int32, v.shape, v.ndim - 1)
    left = jnp.where(at == 0, 0.0, pltpu.roll(v, 1, v.ndim - 1))
    right = jnp.where(at == LY - 1, 0.0, pltpu.roll(v, LY - 1, v.ndim - 1))
    return left + right


def filter_kernel(
    v_hbm, on_hbm, par, u_hbm, acc_ref,
    raw, vt, first, u, ops, acc, ons, relay,
    own_s, on_s, on_r, up_s, up_r, dn_s, dn_r, far_s, far_r, fwd_s, y_s, y_r,
    rel_s, rel_r, gf_s, gf_r, out_s,
):
    c = lax.axis_index("cuts")
    g = lax.axis_index("gz")
    k = lax.rem(g, 2)
    even, odd = k == 0, k == 1
    gp = lax.rem(g + 1, N_GZ)
    gm = lax.rem(g + N_GZ - 1, N_GZ)
    gp2 = lax.rem(g + 2, N_GZ)
    gm2 = lax.rem(g + N_GZ - 2, N_GZ)

    def remote(src, dst, ss, rs, cc, gg):
        return pltpu.make_async_remote_copy(
            src_ref=src, dst_ref=dst, send_sem=ss, recv_sem=rs, device_id=(cc, gg), device_id_type=MESH
        )

    def rows(i):
        return pl.ds(pl.multiple_of(i * XR, XR), XR)

    def own(i):
        return pltpu.make_async_copy(v_hbm.at[:, :, rows(i)], raw.at[i, :, pl.ds(3, 2)], own_s.at[i])

    def up(i):
        return remote(v_hbm.at[:, :, rows(i)], raw.at[i, :, pl.ds(1, 2)], up_s.at[i], up_r.at[i], c, gp)

    def down(i):
        return remote(v_hbm.at[:, :, rows(i)], raw.at[i, :, pl.ds(5, 2)], dn_s.at[i], dn_r.at[i], c, gm)

    def far(i):
        return remote(v_hbm.at[:, pl.ds(1, 1), rows(i)], raw.at[i, :, pl.ds(0, 1)], far_s.at[i], far_r.at[i], c, gp2)

    def forward(i):
        return remote(raw.at[i, :, pl.ds(2, 1)], raw.at[i, :, pl.ds(0, 1)], fwd_s.at[i], far_r.at[i], c, gp)

    def sites(i):
        return pl.ds(1 + i * XR, XR)

    def y_direct(i, lo, n, cc):
        return remote(
            u.at[pl.ds(lo, n), sites(i), pl.ds(0, K)], u.at[pl.ds(lo, n), sites(i), pl.ds(K, K)],
            y_s.at[i], y_r.at[i], cc, g,
        )

    def y_relay(i, lo, n, cc):
        return remote(
            u.at[pl.ds(lo, n), sites(i), pl.ds(0, K)], relay.at[i // 4, pl.ds(lo, n)],
            y_s.at[i], rel_r.at[i // 4], cc, g,
        )

    def relay_on(i, lo, n):
        return remote(
            relay.at[i // 4, pl.ds(lo, n)], u.at[pl.ds(lo, n), sites(i), pl.ds(K, K)],
            rel_s.at[i // 4], y_r.at[i], 3, g,
        )

    def g_forward(i):
        return remote(
            u.at[pl.ds(2, 1), sites(i), pl.ds(K, K)], u.at[pl.ds(0, 1), sites(i), pl.ds(K, K)],
            gf_s.at[i], gf_r.at[i], c, gp,
        )

    def out(i):
        return pltpu.make_async_copy(u.at[pl.ds(1, 2), sites(i)], u_hbm.at[:, rows(i)], out_s.at[i])

    def by_core(act):
        pl.when(even)(lambda: act(0, 3))
        pl.when(odd)(lambda: act(1, 2))

    @pl.loop(0, NC)
    def _(i):
        own(i).start()

    own_on = pltpu.make_async_copy(on_hbm, ons.at[pl.ds(2, 2), pl.ds(8, LX)], on_s.at[0])
    own_on.start()

    barrier = pltpu.get_barrier_semaphore()

    def greet(cc, gg):
        pl.semaphore_signal(barrier, inc=1, device_id=(cc, gg), device_id_type=MESH)

    greet(c, gp)
    greet(c, gm)

    @pl.when(even)
    def _():
        greet(c, gp2)
        greet(c, gm2)

    @pl.when(c > 0)
    def _():
        greet(c - 1, g)

    @pl.when(c < N_CUTS - 1)
    def _():
        greet(c + 1, g)

    @pl.when(c == 4)
    def _():
        greet(6, g)
        greet(7, g)

    @pl.when(c >= 6)
    def _():
        greet(4, g)

    @pl.when(c >= 5)
    def _():
        greet(3, g)

    @pl.when(c == 3)
    def _():
        greet(5, g)
        greet(6, g)
        greet(7, g)

    vt[:, pl.ds(0, 2)] = jnp.zeros((7, 2, K, LY), F32)
    vt[:, pl.ds(LX + 2, 2)] = jnp.zeros((7, 2, K, LY), F32)
    u[:, pl.ds(0, 1)] = jnp.zeros((3, 1, 2 * K, LY), F32)
    u[:, pl.ds(LX + 1, 1)] = jnp.zeros((3, 1, 2 * K, LY), F32)
    ons[:, pl.ds(0, 8)] = jnp.zeros((5, 8, LY), F32)
    ons[:, pl.ds(8 + LX, 8)] = jnp.zeros((5, 8, LY), F32)
    acc[...] = jnp.zeros_like(acc)

    @pl.when(c == N_CUTS - 1)
    def _():
        @pl.loop(0, LX)
        def _(x):
            for z in range(3):
                u[z, 1 + x, pl.ds(K, K)] = jnp.zeros((K, LY), F32)

    def one(p):
        return jnp.where(p, 1, 0)

    partners = 2 + 2 * one(even) + one(c > 0) + one(c < N_CUTS - 1) + one(c >= 6) + one(c >= 5)
    pl.semaphore_wait(barrier, partners + 2 * one(c == 4) + 3 * one(c == 3))

    on_up = remote(on_hbm, ons.at[pl.ds(0, 2), pl.ds(8, LX)], on_s.at[1], on_r.at[0], c, gp)
    on_dn = remote(on_hbm.at[pl.ds(0, 1)], ons.at[pl.ds(4, 1), pl.ds(8, LX)], on_s.at[2], on_r.at[1], c, gm)
    on_up.start()
    on_dn.start()

    @pl.loop(0, NC)
    def _(i):
        up(i).start()
        down(i).start()
        pl.when(even)(lambda: far(i).start())

    ctr, ih, c0, c1, c2 = (par[j] for j in range(5))

    def arrive(i):
        own(i).wait()
        up(i).wait_recv()
        pl.when(even)(lambda: forward(i).start())
        down(i).wait_recv()
        far(i).wait_recv()

        @pl.loop(0, 7)
        def _(z):
            vt[z, pl.ds(2 + i * XR, XR)] = jnp.swapaxes(raw[i, :, z], 0, 1)

    def apply_filter(i):
        @pl.loop(0, XR + 2)
        def _(r):
            x = i * XR - 1 + r
            for z in range(1, 6):
                v = vt[z, 2 + x]
                d = jnp.broadcast_to(ons[z - 1, pl.ds(8 + x, 1), :], (K, LY))
                around = vt[z - 1, 2 + x] + vt[z + 1, 2 + x] + vt[z, 1 + x] + vt[z, 3 + x] + lanes(v)
                first[z - 1, r] = ih * ((d - ctr) * v - around)

        @pl.when(i == 0)
        def _():
            first[:, pl.ds(0, 1)] = jnp.zeros((5, 1, K, LY), F32)

        @pl.when(i == NC - 1)
        def _():
            first[:, pl.ds(XR + 1, 1)] = jnp.zeros((5, 1, K, LY), F32)

        @pl.loop(0, XR)
        def _(r):
            x = i * XR + r
            for z in range(3):
                v = vt[z + 2, 2 + x]
                f = first[z + 1, r + 1]
                d = jnp.broadcast_to(ons[z + 1, pl.ds(8 + x, 1), :], (K, LY))
                around = first[z, r + 1] + first[z + 2, r + 1] + first[z + 1, r] + first[z + 1, r + 2] + lanes(f)
                second = 2.0 * (ih * ((d - ctr) * f - around)) - v
                u[z, 1 + x, pl.ds(0, K)] = c0 * v + c1 * f + c2 * second

    def send(i):
        row = lax.rem(i, 4)
        pl.when((c > 0) & (c != 4))(lambda: by_core(lambda lo, n: y_direct(i, lo, n, c - 1).start()))
        pl.when((c == 4) & (row == 0))(lambda: by_core(lambda lo, n: y_direct(i, lo, n, 3).start()))
        pl.when((c == 4) & (row != 0))(lambda: by_core(lambda lo, n: y_relay(i, lo, n, 4 + row).start()))

    def pass_on(i):
        row = lax.rem(i, 4)

        @pl.when((row != 0) & (c == 4 + row))
        def _():
            def act(lo, n):
                y_relay(i, lo, n, 4 + row).wait_recv()
                relay_on(i, lo, n).start()

            by_core(act)

    def g_arrive(i):
        @pl.when(c < N_CUTS - 1)
        def _():
            by_core(lambda lo, n: y_direct(i, lo, n, c).wait_recv())
            pl.when(even)(lambda: g_forward(i).start())
            pl.when(odd)(lambda: g_forward(i).wait_recv())

    def project(i):
        @pl.loop(0, XR)
        def _(r):
            x = i * XR + r
            for z in range(2):
                at = pl.ds(pl.multiple_of((z * XR + r) * LY, LY), LY)
                mid = u[z + 1, 1 + x]
                d = jnp.broadcast_to(ons[z + 2, pl.ds(8 + x, 1), :], (2 * K, LY))
                w = d * mid - (u[z + 1, x] + u[z + 1, 2 + x] + lanes(mid))
                if z == 0:
                    w = w - 2.0 * (u[0, 1 + x] + u[2, 1 + x])
                hi = mid.astype(BF16)
                w_hi = w.astype(BF16)
                ops[pl.ds(0, 64), at] = hi
                ops[pl.ds(64, 64), at] = (mid - hi.astype(F32)).astype(BF16)
                ops[pl.ds(128, 64), at] = w_hi
                ops[pl.ds(192, 64), at] = (w - w_hi.astype(F32)).astype(BF16)

        acc[...] += lax.dot_general(
            ops[pl.ds(0, 128)], ops[...], (((1,), (1,)), ((), ())), preferred_element_type=F32
        )
        out(i).start()

    own_on.wait()
    on_up.wait()
    on_dn.wait()
    arrive(0)

    @pl.loop(0, NC + LAG + 1)
    def _(i):
        @pl.when(i + 1 < NC)
        def _():
            arrive(i + 1)

        @pl.when(i < NC)
        def _():
            apply_filter(i)
            send(i)

        @pl.when((i >= 1) & (i <= NC))
        def _():
            pass_on(i - 1)

        @pl.when((i >= LAG) & (i < NC + LAG))
        def _():
            g_arrive(i - LAG)

        @pl.when(i >= LAG + 1)
        def _():
            project(i - LAG - 1)

    a = acc[...]
    acc_ref[:, pl.ds(0, 64)] = (a[0:64, 0:64] + a[64:128, 64:128]) + (a[0:64, 64:128] + a[64:128, 0:64])
    acc_ref[:, pl.ds(64, 64)] = (a[0:64, 128:192] + a[64:128, 192:256]) + (a[0:64, 192:256] + a[64:128, 128:192])

    @pl.loop(0, NC)
    def _(i):
        up(i).wait_send()
        down(i).wait_send()

        @pl.when(even)
        def _():
            far(i).wait_send()
            forward(i).wait_send()
            pl.when(c < N_CUTS - 1)(lambda: g_forward(i).wait_send())

        pl.when(c > 0)(lambda: by_core(lambda lo, n: y_direct(i, lo, n, c).wait_send()))
        row = lax.rem(i, 4)
        pl.when((row != 0) & (c == 4 + row))(lambda: by_core(lambda lo, n: relay_on(i, lo, n).wait_send()))
        out(i).wait()


def run_filter(v, onsite, params):
    dma = pltpu.SemaphoreType.DMA
    anyspace = pl.BlockSpec(memory_space=pl.ANY)
    return pl.pallas_call(
        filter_kernel,
        out_shape=(jax.ShapeDtypeStruct((2, LX, 2 * K, LY), F32), jax.ShapeDtypeStruct((2 * K, 128), F32)),
        in_specs=[anyspace, anyspace, pl.BlockSpec(memory_space=pltpu.SMEM)],
        out_specs=(anyspace, pl.BlockSpec(memory_space=pltpu.VMEM)),
        scratch_shapes=[
            pltpu.VMEM((NC, K, 7, XR, LY), F32),
            pltpu.VMEM((7, LX + 4, K, LY), F32),
            pltpu.VMEM((5, XR + 2, K, LY), F32),
            pltpu.VMEM((3, LX + 2, 2 * K, LY), F32),
            pltpu.VMEM((256, 2 * XR * LY), BF16),
            pltpu.VMEM((128, 256), F32),
            pltpu.VMEM((5, LX + 16, LY), F32),
            pltpu.VMEM((NC // 4, 3, XR, K, LY), F32),
            dma((NC,)), dma((3,)), dma((2,)),
            dma((NC,)), dma((NC,)), dma((NC,)), dma((NC,)), dma((NC,)), dma((NC,)), dma((NC,)),
            dma((NC,)), dma((NC,)), dma((NC // 4,)), dma((NC // 4,)), dma((NC,)), dma((NC,)), dma((NC,)),
        ],
        compiler_params=pltpu.CompilerParams(
            collective_id=0, has_side_effects=True, vmem_limit_bytes=60 << 20
        ),
        name="filter",
    )(v, onsite, params)


def solve_kernel(part_ref, linv_ref, proj_ref, half, got, zbuf, full, other, core_s, core_r, x_s, x_r, z_s, z_r, b_s, b_r):
    c = lax.axis_index("cuts")
    g = lax.axis_index("gz")
    k = lax.rem(g, 2)
    hi = lax.rem(g // 2, 2)
    z = g // 4
    mate = g + 1 - 2 * k
    across = g + 2 - 4 * hi

    def remote(src, dst, ss, rs, gg):
        return pltpu.make_async_remote_copy(
            src_ref=src, dst_ref=dst, send_sem=ss, recv_sem=rs, device_id=(c, gg), device_id_type=MESH
        )

    barrier = pltpu.get_barrier_semaphore()
    peers = [lax.rem(g + 4 * n, N_GZ) for n in range(1, 8)]
    for gg in [mate, across] + peers:
        pl.semaphore_signal(barrier, inc=1, device_id=(c, gg), device_id_type=MESH)
    pl.semaphore_wait(barrier, 9)

    mine = pl.ds(pl.multiple_of(32 * k, 32), 32)
    theirs = pl.ds(pl.multiple_of(32 - 32 * k, 32), 32)
    step = remote(part_ref.at[theirs], got.at[0], core_s, core_r, mate)
    step.start()
    step.wait()
    half[0] = part_ref[mine] + got[0]
    step = remote(half.at[0], got.at[1], x_s, x_r, across)
    step.start()
    step.wait()
    total = half[0] + got[1]
    half[1] = total
    zbuf[z] = total
    sends = [remote(half.at[1], zbuf.at[z], z_s.at[n - 1], z_r.at[n - 1], peers[n - 1]) for n in range(1, 8)]
    for s in sends:
        s.start()
    for n in range(1, 8):
        remote(half.at[1], zbuf.at[lax.rem(z - n + 8, 8)], z_s.at[n - 1], z_r.at[n - 1], peers[n - 1]).wait_recv()
    for s in sends:
        s.wait_send()
    t = [zbuf[n] for n in range(8)]
    full[mine] = ((t[0] + t[1]) + (t[2] + t[3])) + ((t[4] + t[5]) + (t[6] + t[7]))
    step = remote(full.at[mine], full.at[mine], b_s, b_r, mate)
    step.start()
    remote(full.at[theirs], full.at[theirs], b_s, b_r, mate).wait_recv()
    step.wait_send()

    both = full[...] * (1.0 / SITES)
    sub = lax.broadcasted_iota(jnp.int32, (64, 128), 0)
    lane = lax.broadcasted_iota(jnp.int32, (64, 128), 1)
    m = both[:, 64:128]
    a = jnp.where(lane < 64, both, 0.0) + jnp.where(lane == sub, 0.25, 0.0) + jnp.where(lane == sub + 64, 1.0, 0.0)
    for i in range(63):
        row = a[i : i + 1, :]
        scaled = row / row[:, i : i + 1]
        lo = (i + 1) // 8 * 8
        low = a[lo:, :]
        col = jnp.where(sub[lo:, :] > i, jnp.broadcast_to(low[:, i : i + 1], low.shape), 0.0)
        low = low - col * scaled
        a = low if lo == 0 else jnp.concatenate([a[:lo, :], low], 0)
    diag = jnp.sum(jnp.where(lane == sub, a, 0.0), axis=1, keepdims=True)
    linv = a[:, 64:128] * (1.0 / jnp.sqrt(diag))
    linv_ref[...] = linv

    def exact(p, q, dims):
        return lax.dot_general(p, q, (dims, ((), ())), precision=lax.Precision.HIGHEST, preferred_element_type=F32)

    right = exact(m, linv, ((1,), (1,)))
    p = exact(linv, right, ((1,), (0,)))
    proj_ref[0] = 0.5 * (p + p.T)


def run_solve(part):
    dma = pltpu.SemaphoreType.DMA
    vm = pl.BlockSpec(memory_space=pltpu.VMEM)
    return pl.pallas_call(
        solve_kernel,
        out_shape=(jax.ShapeDtypeStruct((64, 64), F32), jax.ShapeDtypeStruct((1, 64, 64), F32)),
        in_specs=[vm],
        out_specs=(vm, vm),
        scratch_shapes=[
            pltpu.VMEM((2, 32, 128), F32), pltpu.VMEM((2, 32, 128), F32), pltpu.VMEM((8, 32, 128), F32),
            pltpu.VMEM((64, 128), F32), pltpu.VMEM((64, 128), F32),
            dma, dma, dma, dma, dma((7,)), dma((7,)), dma, dma,
        ],
        compiler_params=pltpu.CompilerParams(collective_id=1, has_side_effects=True),
        name="solve",
    )(part)


XB = 16


def basis_kernel(linv_ref, u_ref, out_ref, tmp):
    linv = linv_ref[...]
    hi = linv.astype(BF16)
    lo = (linv - hi.astype(F32)).astype(BF16)
    left = jnp.concatenate([hi, lo, hi], 1)
    for x in range(0, XB, 2):
        right = []
        for s in range(2):
            t = u_ref[0, x + s]
            t_hi = t.astype(BF16)
            t_lo = (t - t_hi.astype(F32)).astype(BF16)
            right.append(jnp.concatenate([t_hi, t_hi, t_lo], 0))
        got = jnp.dot(left, jnp.concatenate(right, 1), preferred_element_type=F32)
        tmp[x] = got[:, :LY]
        tmp[x + 1] = got[:, LY:]
    for x in range(0, XB, 8):
        out_ref[0, :, 0, pl.ds(x, 8)] = jnp.swapaxes(tmp[pl.ds(x, 8)], 0, 1)


def run_basis(linv, u):
    return pl.pallas_call(
        basis_kernel,
        out_shape=jax.ShapeDtypeStruct((1, 2 * K, 2, LX, LY), F32),
        grid=(2, LX // XB),
        in_specs=[
            pl.BlockSpec((64, 64), lambda z, x: (0, 0)),
            pl.BlockSpec((1, XB, 2 * K, LY), lambda z, x: (z, x, 0, 0)),
        ],
        out_specs=pl.BlockSpec((1, 2 * K, 1, XB, LY), lambda z, x: (0, 0, z, x, 0)),
        scratch_shapes=[pltpu.VMEM((XB, 2 * K, LY), F32)],
        compiler_params=pltpu.CompilerParams(vmem_limit_bytes=32 << 20),
        name="basis",
    )(linv, u)


def body(vectors, onsite, center, inv_half, cheb_coef):
    params = jnp.concatenate([center, inv_half, cheb_coef[0]])
    u, part = run_filter(vectors[0], onsite, params)
    linv, projected = run_solve(part)
    return run_basis(linv, u), projected


def solution(mesh):
    in_specs = (
        P("cuts", None, "gz", None, None),
        P("gz", None, None),
        P("cuts"),
        P("cuts"),
        P("cuts", None),
    )
    out_specs = (P("cuts", None, "gz", None, None), P("cuts", None, None))
    return jax.shard_map(body, mesh=mesh, in_specs=in_specs, out_specs=out_specs, check_vma=False)
```

```python
import functools

import jax
import jax.numpy as jnp
from jax import lax
from jax.experimental import pallas as pl
from jax.experimental.pallas import tpu as pltpu
from jax.sharding import PartitionSpec as P

MESH = pl.DeviceIdType.MESH
K = 32
LX = 128
LY = 128
XR = 8
NC = LX // XR
LAG = 3
LAG_FAR = 6
AHEAD = 3
N_CUTS = 8
N_GZ = 32
SITES = 64 * 128 * 128
F32 = jnp.float32
BF16 = jnp.bfloat16


def lanes(v):
    at = lax.broadcasted_iota(jnp.int32, v.shape, v.ndim - 1)
    left = jnp.where(at == 0, 0.0, pltpu.roll(v, 1, v.ndim - 1))
    right = jnp.where(at == LY - 1, 0.0, pltpu.roll(v, LY - 1, v.ndim - 1))
    return left + right


def filter_kernel(
    v_hbm, on_hbm, ctr_ref, ih_ref, cheb, f_hbm, g_hbm, acc_ref,
    mine, below, above, far_in, vt, first, fs, gs, ops, acc, ons, relay,
    own_s, on_s, on_r, up_s, up_r, dn_s, dn_r, far_s, far_r, fwd_s, y_s, y_r,
    rel_s, rel_r, gf_s, gf_r, out_s,
):
    c = lax.axis_index("cuts")
    g = lax.axis_index("gz")
    k = lax.rem(g, 2)
    even, odd = k == 0, k == 1
    gp = lax.rem(g + 1, N_GZ)
    gm = lax.rem(g + N_GZ - 1, N_GZ)
    gp2 = lax.rem(g + 2, N_GZ)
    gm2 = lax.rem(g + N_GZ - 2, N_GZ)

    def remote(src, dst, ss, rs, cc, gg):
        return pltpu.make_async_remote_copy(
            src_ref=src, dst_ref=dst, send_sem=ss, recv_sem=rs, device_id=(cc, gg), device_id_type=MESH
        )

    def rows(i):
        return pl.ds(pl.multiple_of(i * XR, XR), XR)

    def own(i, z):
        return pltpu.make_async_copy(v_hbm.at[:, z, rows(i)], mine.at[i, z], own_s.at[z, i])

    def up(i):
        return remote(mine.at[i], below.at[i], up_s.at[i], up_r.at[i], c, gp)

    def down(i):
        return remote(mine.at[i], above.at[i], dn_s.at[i], dn_r.at[i], c, gm)

    def far(i):
        return remote(mine.at[i, 1], far_in.at[i], far_s.at[i], far_r.at[i], c, gp2)

    def forward(i):
        return remote(below.at[i, 1], far_in.at[i], fwd_s.at[i], far_r.at[i], c, gp)

    def y_direct(i, lo, n, cc):
        return remote(fs.at[1 + i, pl.ds(lo, n)], gs.at[1 + i, pl.ds(lo, n)], y_s.at[i], y_r.at[i], cc, g)

    def y_relay(i, lo, n, cc):
        return remote(fs.at[1 + i, pl.ds(lo, n)], relay.at[i // 4, pl.ds(lo, n)], y_s.at[i], rel_r.at[i // 4], cc, g)

    def relay_on(i, lo, n):
        return remote(relay.at[i // 4, pl.ds(lo, n)], gs.at[1 + i, pl.ds(lo, n)], rel_s.at[i // 4], y_r.at[i], 3, g)

    def relay_twice(i, lo, n):
        return remote(
            relay.at[i // 4, pl.ds(lo, n)], relay.at[i // 4, pl.ds(lo, n)], rel_s.at[i // 4], rel_r.at[i // 4], 2, g
        )

    def g_forward(i):
        return remote(gs.at[1 + i, 2], gs.at[1 + i, 0], gf_s.at[i], gf_r.at[i], c, gp)

    def out_f(i):
        return pltpu.make_async_copy(fs.at[1 + i, pl.ds(1, 2)], f_hbm.at[i], out_s.at[0, i])

    def out_g(i):
        return pltpu.make_async_copy(gs.at[1 + i, pl.ds(1, 2)], g_hbm.at[i], out_s.at[1, i])

    def row_of(i):
        m = lax.rem(i, 4)
        return jnp.where(m == 0, 1, jnp.where(m == 1, 3, jnp.where(m == 2, 2, 0)))

    def row_of(i):
        m = lax.rem(i, 4)
        return jnp.where(m == 0, 1, jnp.where(m == 1, 3, jnp.where(m == 2, 2, 0)))

    def by_core(act):
        pl.when(even)(lambda: act(0, 3))
        pl.when(odd)(lambda: act(1, 2))

    @pl.loop(0, NC)
    def _(i):
        own(i, 0).start()
        own(i, 1).start()

    own_on = pltpu.make_async_copy(on_hbm, ons.at[pl.ds(2, 2), pl.ds(8, LX)], on_s.at[0])
    own_on.start()

    barrier = pltpu.get_barrier_semaphore()

    def greet(cc, gg):
        pl.semaphore_signal(barrier, inc=1, device_id=(cc, gg), device_id_type=MESH)

    greet(c, gp)
    greet(c, gm)

    @pl.when(even)
    def _():
        greet(c, gp2)
        greet(c, gm2)

    @pl.when(c > 0)
    def _():
        greet(c - 1, g)

    @pl.when(c < N_CUTS - 1)
    def _():
        greet(c + 1, g)

    @pl.when(c == 4)
    def _():
        greet(6, g)
        greet(7, g)

    @pl.when(c >= 6)
    def _():
        greet(4, g)
        greet(3, g)

    @pl.when(c == 3)
    def _():
        greet(6, g)
        greet(7, g)

    pl.when(c == 5)(lambda: greet(2, g))
    pl.when(c == 2)(lambda: greet(5, g))

    vt[:, pl.ds(0, 2)] = jnp.zeros((7, 2, K, LY), F32)
    vt[:, pl.ds(LX + 2, 2)] = jnp.zeros((7, 2, K, LY), F32)
    for edge in (fs, gs):
        edge[0, :, 7] = jnp.zeros((3, K, LY), F32)
        edge[NC + 1, :, 0] = jnp.zeros((3, K, LY), F32)
    ons[:, pl.ds(0, 8)] = jnp.zeros((5, 8, LY), F32)
    ons[:, pl.ds(8 + LX, 8)] = jnp.zeros((5, 8, LY), F32)
    acc[...] = jnp.zeros_like(acc)

    @pl.when(c == N_CUTS - 1)
    def _():
        @pl.loop(0, LX)
        def _(x):
            for z in range(3):
                gs[1 + x // XR, z, lax.rem(x, XR)] = jnp.zeros((K, LY), F32)

    def one(p):
        return jnp.where(p, 1, 0)

    partners = 2 + 2 * one(even) + one(c > 0) + one(c < N_CUTS - 1) + one(c == 5) + one(c == 2)
    pl.semaphore_wait(barrier, partners + 2 * (one(c >= 6) + one(c == 4) + one(c == 3)))

    on_up = remote(on_hbm, ons.at[pl.ds(0, 2), pl.ds(8, LX)], on_s.at[1], on_r.at[0], c, gp)
    on_dn = remote(on_hbm.at[pl.ds(0, 1)], ons.at[pl.ds(4, 1), pl.ds(8, LX)], on_s.at[2], on_r.at[1], c, gm)
    on_up.start()
    on_dn.start()

    def v_send(i):
        own(i, 0).wait()
        own(i, 1).wait()
        up(i).start()
        down(i).start()
        pl.when(even)(lambda: far(i).start())

    pl.loop(0, AHEAD)(v_send)

    ctr, ih, c0, c1, c2 = ctr_ref[0], ih_ref[0], cheb[0, 0], cheb[0, 1], cheb[0, 2]

    def arrive(i):
        up(i).wait_recv()
        pl.when(even)(lambda: forward(i).start())
        down(i).wait_recv()
        far(i).wait_recv()
        to = pl.ds(2 + i * XR, XR)
        vt[0, to] = jnp.swapaxes(far_in[i], 0, 1)

        @pl.loop(0, 2)
        def _(z):
            vt[1 + z, to] = jnp.swapaxes(below[i, z], 0, 1)
            vt[3 + z, to] = jnp.swapaxes(mine[i, z], 0, 1)
            vt[5 + z, to] = jnp.swapaxes(above[i, z], 0, 1)

    def apply_filter(i):
        @pl.loop(0, XR + 2)
        def _(r):
            x = i * XR - 1 + r
            for z in range(1, 6):
                v = vt[z, 2 + x]
                d = jnp.broadcast_to(ons[z - 1, pl.ds(8 + x, 1), :], (K, LY))
                around = vt[z - 1, 2 + x] + vt[z + 1, 2 + x] + vt[z, 1 + x] + vt[z, 3 + x] + lanes(v)
                first[z - 1, r] = ih * ((d - ctr) * v - around)

        @pl.when(i == 0)
        def _():
            first[:, pl.ds(0, 1)] = jnp.zeros((5, 1, K, LY), F32)

        @pl.when(i == NC - 1)
        def _():
            first[:, pl.ds(XR + 1, 1)] = jnp.zeros((5, 1, K, LY), F32)

        @pl.loop(0, XR)
        def _(r):
            x = i * XR + r
            for z in range(3):
                v = vt[z + 2, 2 + x]
                f = first[z + 1, r + 1]
                d = jnp.broadcast_to(ons[z + 1, pl.ds(8 + x, 1), :], (K, LY))
                around = first[z, r + 1] + first[z + 2, r + 1] + first[z + 1, r] + first[z + 1, r + 2] + lanes(f)
                second = 2.0 * (ih * ((d - ctr) * f - around)) - v
                fs[1 + i, z, r] = c0 * v + c1 * f + c2 * second

    def send(i):
        row = row_of(i)
        pl.when((c > 0) & (c != 4))(lambda: by_core(lambda lo, n: y_direct(i, lo, n, c - 1).start()))
        pl.when((c == 4) & (row == 0))(lambda: by_core(lambda lo, n: y_direct(i, lo, n, 3).start()))
        pl.when((c == 4) & (row != 0))(lambda: by_core(lambda lo, n: y_relay(i, lo, n, 4 + row).start()))

    def pass_on(i, onward, here):
        @pl.when(here)
        def _():
            def act(lo, n):
                y_relay(i, lo, n, c).wait_recv()
                onward(i, lo, n).start()

            by_core(act)

    def pass_ons(i):
        row = row_of(i)
        pass_on(i, relay_on, (row >= 2) & (c == 4 + row))
        pass_on(i, relay_twice, (row == 1) & (c == 5))

    def pass_last(i):
        pass_on(i, relay_on, (row_of(i) == 1) & (c == 2))

    def g_arrive(i):
        @pl.when(c < N_CUTS - 1)
        def _():
            by_core(lambda lo, n: y_direct(i, lo, n, c).wait_recv())
            pl.when(even)(lambda: g_forward(i).start())
            pl.when(odd)(lambda: g_forward(i).wait_recv())

    def project(i):
        @pl.loop(0, XR)
        def _(r):
            x = i * XR + r
            before, after = x + XR - 1, x + XR + 1
            for z in range(2):
                at = pl.ds(pl.multiple_of((z * XR + r) * LY, LY), LY)
                d = jnp.broadcast_to(ons[z + 2, pl.ds(8 + x, 1), :], (K, LY))
                for part, field in enumerate((fs, gs)):
                    mid = field[1 + i, z + 1, r]
                    around = field[before // XR, z + 1, lax.rem(before, XR)] + field[after // XR, z + 1, lax.rem(after, XR)]
                    w = d * mid - (around + lanes(mid))
                    if z == 0:
                        w = w - 2.0 * (field[1 + i, 0, r] + field[1 + i, 2, r])
                    hi = mid.astype(BF16)
                    w_hi = w.astype(BF16)
                    ops[pl.ds(part * K, K), at] = hi
                    ops[pl.ds(64 + part * K, K), at] = (mid - hi.astype(F32)).astype(BF16)
                    ops[pl.ds(128 + part * K, K), at] = w_hi
                    ops[pl.ds(192 + part * K, K), at] = (w - w_hi.astype(F32)).astype(BF16)

        acc[...] += lax.dot_general(
            ops[pl.ds(0, 128)], ops[...], (((1,), (1,)), ((), ())), preferred_element_type=F32
        )
        out_f(i).start()
        out_g(i).start()

    own_on.wait()
    on_up.wait()
    on_dn.wait()
    arrive(0)

    lag = jnp.where(c == 3, LAG_FAR, LAG)

    @pl.loop(0, NC + LAG_FAR + 1)
    def _(i):
        @pl.when(i + 1 < NC)
        def _():
            arrive(i + 1)
            pl.when(i + AHEAD < NC)(lambda: v_send(i + AHEAD))

        @pl.when(i < NC - 1)
        def _():
            @pl.loop(i, jnp.where(i == NC - 2, NC, i + 1))
            def _(j):
                apply_filter(j)
                send(j)

        @pl.when((i >= 1) & (i <= NC))
        def _():
            pass_ons(i - 1)

        @pl.when((i >= 2) & (i <= NC + 1))
        def _():
            pass_last(i - 2)

        @pl.when((i >= lag) & (i < NC + lag))
        def _():
            g_arrive(i - lag)

        @pl.when((i >= lag + 1) & (i < NC + lag + 1))
        def _():
            project(i - lag - 1)

    a = acc[...]
    acc_ref[:, pl.ds(0, 64)] = (a[0:64, 0:64] + a[64:128, 64:128]) + (a[0:64, 64:128] + a[64:128, 0:64])
    acc_ref[:, pl.ds(64, 64)] = (a[0:64, 128:192] + a[64:128, 192:256]) + (a[0:64, 192:256] + a[64:128, 128:192])

    @pl.loop(0, NC)
    def _(i):
        up(i).wait_send()
        down(i).wait_send()

        @pl.when(even)
        def _():
            far(i).wait_send()
            forward(i).wait_send()
            pl.when(c < N_CUTS - 1)(lambda: g_forward(i).wait_send())

        pl.when(c > 0)(lambda: by_core(lambda lo, n: y_direct(i, lo, n, c).wait_send()))
        row = row_of(i)
        passed = (row >= 1) & ((c == 4 + row) | ((c == 2) & (row == 1)))
        pl.when(passed)(lambda: by_core(lambda lo, n: relay_on(i, lo, n).wait_send()))
        out_f(i).wait()
        out_g(i).wait()


def run_filter(v, onsite, center, inv_half, cheb):
    dma = pltpu.SemaphoreType.DMA
    anyspace = pl.BlockSpec(memory_space=pl.ANY)
    return pl.pallas_call(
        filter_kernel,
        out_shape=(
            jax.ShapeDtypeStruct((NC, 2, XR, K, LY), F32),
            jax.ShapeDtypeStruct((NC, 2, XR, K, LY), F32),
            jax.ShapeDtypeStruct((2 * K, 128), F32),
        ),
        in_specs=[anyspace, anyspace] + [pl.BlockSpec(memory_space=pltpu.SMEM)] * 3,
        out_specs=(anyspace, anyspace, pl.BlockSpec(memory_space=pltpu.VMEM)),
        scratch_shapes=[
            pltpu.VMEM((NC, 2, K, XR, LY), F32),
            pltpu.VMEM((NC, 2, K, XR, LY), F32),
            pltpu.VMEM((NC, 2, K, XR, LY), F32),
            pltpu.VMEM((NC, K, XR, LY), F32),
            pltpu.VMEM((7, LX + 4, K, LY), F32),
            pltpu.VMEM((5, XR + 2, K, LY), F32),
            pltpu.VMEM((NC + 2, 3, XR, K, LY), F32),
            pltpu.VMEM((NC + 2, 3, XR, K, LY), F32),
            pltpu.VMEM((256, 2 * XR * LY), BF16),
            pltpu.VMEM((128, 256), F32),
            pltpu.VMEM((5, LX + 16, LY), F32),
            pltpu.VMEM((NC // 4, 3, XR, K, LY), F32),
            dma((2, NC)), dma((3,)), dma((2,)),
            dma((NC,)), dma((NC,)), dma((NC,)), dma((NC,)), dma((NC,)), dma((NC,)), dma((NC,)),
            dma((NC,)), dma((NC,)), dma((NC // 4,)), dma((NC // 4,)), dma((NC,)), dma((NC,)), dma((2, NC)),
        ],
        compiler_params=pltpu.CompilerParams(
            collective_id=0, has_side_effects=True, vmem_limit_bytes=60 << 20
        ),
        name="filter",
    )(v, onsite, center, inv_half, cheb)


def solve_kernel(part_ref, linv_ref, proj_ref, half, got, zbuf, full, other, core_s, core_r, x_s, x_r, z_s, z_r, b_s, b_r):
    c = lax.axis_index("cuts")
    g = lax.axis_index("gz")
    k = lax.rem(g, 2)
    hi = lax.rem(g // 2, 2)
    z = g // 4
    mate = g + 1 - 2 * k
    across = g + 2 - 4 * hi

    def remote(src, dst, ss, rs, gg):
        return pltpu.make_async_remote_copy(
            src_ref=src, dst_ref=dst, send_sem=ss, recv_sem=rs, device_id=(c, gg), device_id_type=MESH
        )

    barrier = pltpu.get_barrier_semaphore()
    peers = [lax.rem(g + 4 * n, N_GZ) for n in range(1, 8)]
    for gg in [mate, across] + peers:
        pl.semaphore_signal(barrier, inc=1, device_id=(c, gg), device_id_type=MESH)
    pl.semaphore_wait(barrier, 9)

    mine = pl.ds(pl.multiple_of(32 * k, 32), 32)
    theirs = pl.ds(pl.multiple_of(32 - 32 * k, 32), 32)
    step = remote(part_ref.at[theirs], got.at[0], core_s, core_r, mate)
    step.start()
    step.wait()
    half[0] = part_ref[mine] + got[0]
    step = remote(half.at[0], got.at[1], x_s, x_r, across)
    step.start()
    step.wait()
    total = half[0] + got[1]
    half[1] = total
    zbuf[z] = total
    sends = [remote(half.at[1], zbuf.at[z], z_s.at[n - 1], z_r.at[n - 1], peers[n - 1]) for n in range(1, 8)]
    for s in sends:
        s.start()
    for n in range(1, 8):
        remote(half.at[1], zbuf.at[lax.rem(z - n + 8, 8)], z_s.at[n - 1], z_r.at[n - 1], peers[n - 1]).wait_recv()
    for s in sends:
        s.wait_send()
    t = [zbuf[n] for n in range(8)]
    full[mine] = ((t[0] + t[1]) + (t[2] + t[3])) + ((t[4] + t[5]) + (t[6] + t[7]))
    step = remote(full.at[mine], full.at[mine], b_s, b_r, mate)
    step.start()
    remote(full.at[theirs], full.at[theirs], b_s, b_r, mate).wait_recv()
    step.wait_send()

    both = full[...] * (1.0 / SITES)
    sub = lax.broadcasted_iota(jnp.int32, (64, 128), 0)
    lane = lax.broadcasted_iota(jnp.int32, (64, 128), 1)
    m = both[:, 64:128]
    a = jnp.where(lane < 64, both, 0.0) + jnp.where(lane == sub, 0.25, 0.0) + jnp.where(lane == sub + 64, 1.0, 0.0)
    for i in range(63):
        row = a[i : i + 1, :]
        scaled = row / row[:, i : i + 1]
        lo = (i + 1) // 8 * 8
        low = a[lo:, :]
        col = jnp.where(sub[lo:, :] > i, jnp.broadcast_to(low[:, i : i + 1], low.shape), 0.0)
        low = low - col * scaled
        a = low if lo == 0 else jnp.concatenate([a[:lo, :], low], 0)
    diag = jnp.sum(jnp.where(lane == sub, a, 0.0), axis=1, keepdims=True)
    linv = a[:, 64:128] * (1.0 / jnp.sqrt(diag))
    linv_ref[...] = linv

    def exact(p, q, dims):
        return lax.dot_general(p, q, (dims, ((), ())), precision=lax.Precision.HIGHEST, preferred_element_type=F32)

    right = exact(m, linv, ((1,), (1,)))
    p = exact(linv, right, ((1,), (0,)))
    proj_ref[0] = 0.5 * (p + p.T)


def run_solve(part):
    dma = pltpu.SemaphoreType.DMA
    vm = pl.BlockSpec(memory_space=pltpu.VMEM)
    return pl.pallas_call(
        solve_kernel,
        out_shape=(jax.ShapeDtypeStruct((64, 64), F32), jax.ShapeDtypeStruct((1, 64, 64), F32)),
        in_specs=[vm],
        out_specs=(vm, vm),
        scratch_shapes=[
            pltpu.VMEM((2, 32, 128), F32), pltpu.VMEM((2, 32, 128), F32), pltpu.VMEM((8, 32, 128), F32),
            pltpu.VMEM((64, 128), F32), pltpu.VMEM((64, 128), F32),
            dma, dma, dma, dma, dma((7,)), dma((7,)), dma, dma,
        ],
        compiler_params=pltpu.CompilerParams(collective_id=1, has_side_effects=True),
        name="solve",
    )(part)


def basis_kernel(linv_ref, p_ref, f_ref, g_ref, out_ref, proj_ref, tmp):
    proj_ref[...] = p_ref[...]
    linv = linv_ref[...]
    hi = linv.astype(BF16)
    lo = (linv - hi.astype(F32)).astype(BF16)
    left = jnp.concatenate([hi, lo, hi], 1)
    for n in range(2):
        for z in range(2):
            for x in range(0, XR, 2):
                right = []
                for s in range(2):
                    t = jnp.concatenate([f_ref[n, z, x + s], g_ref[n, z, x + s]], 0)
                    t_hi = t.astype(BF16)
                    t_lo = (t - t_hi.astype(F32)).astype(BF16)
                    right.append(jnp.concatenate([t_hi, t_hi, t_lo], 0))
                got = jnp.dot(left, jnp.concatenate(right, 1), preferred_element_type=F32)
                tmp[x] = got[:, :LY]
                tmp[x + 1] = got[:, LY:]
            out_ref[0, :, z, pl.ds(n * XR, XR)] = jnp.swapaxes(tmp[...], 0, 1)


def run_basis(linv, p, f, g):
    small = pl.BlockSpec((1, 64, 64), lambda i: (0, 0, 0))
    half = pl.BlockSpec((2, 2, XR, K, LY), lambda i: (i, 0, 0, 0, 0))
    return pl.pallas_call(
        basis_kernel,
        out_shape=(jax.ShapeDtypeStruct((1, 2 * K, 2, LX, LY), F32), jax.ShapeDtypeStruct((1, 64, 64), F32)),
        grid=(NC // 2,),
        in_specs=[pl.BlockSpec((64, 64), lambda i: (0, 0)), small, half, half],
        out_specs=(pl.BlockSpec((1, 2 * K, 2, 2 * XR, LY), lambda i: (0, 0, 0, i, 0)), small),
        scratch_shapes=[pltpu.VMEM((XR, 2 * K, LY), F32)],
        compiler_params=pltpu.CompilerParams(vmem_limit_bytes=60 << 20),
        name="basis",
    )(linv, p, f, g)


def body(vectors, onsite, center, inv_half, cheb_coef):
    f, g, part = run_filter(vectors[0], onsite, center, inv_half, cheb_coef)
    linv, projected = run_solve(part)
    return run_basis(linv, projected, f, g)


def solution(mesh):
    in_specs = (
        P("cuts", None, "gz", None, None),
        P("gz", None, None),
        P("cuts"),
        P("cuts"),
        P("cuts", None),
    )
    out_specs = (P("cuts", None, "gz", None, None), P("cuts", None, None))
    return jax.shard_map(body, mesh=mesh, in_specs=in_specs, out_specs=out_specs, check_vma=False)
```

```python
import functools

import jax
import jax.numpy as jnp
from jax import lax
from jax.experimental import pallas as pl
from jax.experimental.pallas import tpu as pltpu
from jax.sharding import PartitionSpec as P

MESH = pl.DeviceIdType.MESH
K = 32
LX = 128
LY = 128
XR = 8
NC = LX // XR
LAG = 3
LAG_FAR = 6
AHEAD = 3
N_CUTS = 8
N_GZ = 32
SITES = 64 * 128 * 128
F32 = jnp.float32
BF16 = jnp.bfloat16


def lanes(v):
    at = lax.broadcasted_iota(jnp.int32, v.shape, v.ndim - 1)
    left = jnp.where(at == 0, 0.0, pltpu.roll(v, 1, v.ndim - 1))
    right = jnp.where(at == LY - 1, 0.0, pltpu.roll(v, LY - 1, v.ndim - 1))
    return left + right


def solve(c, g, remote, part, linv_ref, proj_ref, half, got, zbuf, full, core_s, core_r, x_s, x_r, z_s, z_r, b_s, b_r):
    k = lax.rem(g, 2)
    z = g // 4
    mate = g + 1 - 2 * k
    across = g + 2 - 4 * lax.rem(g // 2, 2)
    peers = [lax.rem(g + 4 * n, N_GZ) for n in range(1, 8)]

    my_rows = pl.ds(pl.multiple_of(32 * k, 32), 32)
    theirs = pl.ds(pl.multiple_of(32 - 32 * k, 32), 32)
    step = remote(part.at[theirs], got.at[0], core_s, core_r, c, mate)
    step.start()
    step.wait()
    half[0] = part[my_rows] + got[0]
    step = remote(half.at[0], got.at[1], x_s, x_r, c, across)
    step.start()
    step.wait()
    total = half[0] + got[1]
    half[1] = total
    zbuf[z] = total
    sends = [remote(half.at[1], zbuf.at[z], z_s.at[n - 1], z_r.at[n - 1], c, peers[n - 1]) for n in range(1, 8)]
    for s in sends:
        s.start()
    for n in range(1, 8):
        remote(half.at[1], zbuf.at[lax.rem(z - n + 8, 8)], z_s.at[n - 1], z_r.at[n - 1], c, peers[n - 1]).wait_recv()
    for s in sends:
        s.wait_send()
    t = [zbuf[n] for n in range(8)]
    full[my_rows] = ((t[0] + t[1]) + (t[2] + t[3])) + ((t[4] + t[5]) + (t[6] + t[7]))
    step = remote(full.at[my_rows], full.at[my_rows], b_s, b_r, c, mate)
    step.start()
    remote(full.at[theirs], full.at[theirs], b_s, b_r, c, mate).wait_recv()
    step.wait_send()

    both = full[...] * (1.0 / SITES)
    sub = lax.broadcasted_iota(jnp.int32, (64, 128), 0)
    lane = lax.broadcasted_iota(jnp.int32, (64, 128), 1)
    m = both[:, 64:128]
    a = jnp.where(lane < 64, both, 0.0) + jnp.where(lane == sub, 0.25, 0.0) + jnp.where(lane == sub + 64, 1.0, 0.0)
    for i in range(63):
        row = a[i : i + 1, :]
        scaled = row / row[:, i : i + 1]
        lo = (i + 1) // 8 * 8
        low = a[lo:, :]
        col = jnp.where(sub[lo:, :] > i, jnp.broadcast_to(low[:, i : i + 1], low.shape), 0.0)
        low = low - col * scaled
        a = low if lo == 0 else jnp.concatenate([a[:lo, :], low], 0)
    diag = jnp.sum(jnp.where(lane == sub, a, 0.0), axis=1, keepdims=True)
    linv = a[:, 64:128] * (1.0 / jnp.sqrt(diag))
    linv_ref[...] = linv

    def exact(p, q, dims):
        return lax.dot_general(p, q, (dims, ((), ())), precision=lax.Precision.HIGHEST, preferred_element_type=F32)

    right = exact(m, linv, ((1,), (1,)))
    p = exact(linv, right, ((1,), (0,)))
    proj_ref[0] = 0.5 * (p + p.T)


def filter_kernel(
    v_hbm, on_hbm, ctr_ref, ih_ref, cheb, f_hbm, g_hbm, linv_ref, proj_ref,
    mine, below, above, far_in, vt, first, fs, gs, ops, acc, ons, relay,
    own_s, on_s, on_r, up_s, up_r, dn_s, dn_r, far_s, far_r, fwd_s, y_s, y_r,
    rel_s, rel_r, gf_s, gf_r, out_s, part, *solve_scratch,
):
    c = lax.axis_index("cuts")
    g = lax.axis_index("gz")
    k = lax.rem(g, 2)
    even, odd = k == 0, k == 1
    gp = lax.rem(g + 1, N_GZ)
    gm = lax.rem(g + N_GZ - 1, N_GZ)
    gp2 = lax.rem(g + 2, N_GZ)
    gm2 = lax.rem(g + N_GZ - 2, N_GZ)

    def remote(src, dst, ss, rs, cc, gg):
        return pltpu.make_async_remote_copy(
            src_ref=src, dst_ref=dst, send_sem=ss, recv_sem=rs, device_id=(cc, gg), device_id_type=MESH
        )

    def rows(i):
        return pl.ds(pl.multiple_of(i * XR, XR), XR)

    def own(i, z):
        return pltpu.make_async_copy(v_hbm.at[:, z, rows(i)], mine.at[i, z], own_s.at[z, i])

    def up(i):
        return remote(mine.at[i], below.at[i], up_s.at[i], up_r.at[i], c, gp)

    def down(i):
        return remote(mine.at[i], above.at[i], dn_s.at[i], dn_r.at[i], c, gm)

    def far(i):
        return remote(mine.at[i, 1], far_in.at[i], far_s.at[i], far_r.at[i], c, gp2)

    def forward(i):
        return remote(below.at[i, 1], far_in.at[i], fwd_s.at[i], far_r.at[i], c, gp)

    def y_direct(i, lo, n, cc):
        return remote(fs.at[1 + i, pl.ds(lo, n)], gs.at[1 + i, pl.ds(lo, n)], y_s.at[i], y_r.at[i], cc, g)

    def y_relay(i, lo, n, cc):
        return remote(fs.at[1 + i, pl.ds(lo, n)], relay.at[i // 4, pl.ds(lo, n)], y_s.at[i], rel_r.at[i // 4], cc, g)

    def relay_on(i, lo, n):
        return remote(relay.at[i // 4, pl.ds(lo, n)], gs.at[1 + i, pl.ds(lo, n)], rel_s.at[i // 4], y_r.at[i], 3, g)

    def relay_twice(i, lo, n):
        return remote(
            relay.at[i // 4, pl.ds(lo, n)], relay.at[i // 4, pl.ds(lo, n)], rel_s.at[i // 4], rel_r.at[i // 4], 2, g
        )

    def g_forward(i):
        return remote(gs.at[1 + i, 2], gs.at[1 + i, 0], gf_s.at[i], gf_r.at[i], c, gp)

    def out_f(i):
        return pltpu.make_async_copy(fs.at[1 + i, pl.ds(1, 2)], f_hbm.at[i], out_s.at[0, i])

    def out_g(i):
        return pltpu.make_async_copy(gs.at[1 + i, pl.ds(1, 2)], g_hbm.at[i], out_s.at[1, i])

    def row_of(i):
        m = lax.rem(i, 4)
        return jnp.where(m == 0, 1, jnp.where(m == 1, 3, jnp.where(m == 2, 2, 0)))

    def row_of(i):
        m = lax.rem(i, 4)
        return jnp.where(m == 0, 1, jnp.where(m == 1, 3, jnp.where(m == 2, 2, 0)))

    def by_core(act):
        pl.when(even)(lambda: act(0, 3))
        pl.when(odd)(lambda: act(1, 2))

    @pl.loop(0, NC)
    def _(i):
        own(i, 0).start()
        own(i, 1).start()

    own_on = pltpu.make_async_copy(on_hbm, ons.at[pl.ds(2, 2), pl.ds(8, LX)], on_s.at[0])
    own_on.start()

    barrier = pltpu.get_barrier_semaphore()

    def greet(cc, gg):
        pl.semaphore_signal(barrier, inc=1, device_id=(cc, gg), device_id_type=MESH)

    greet(c, gp)
    greet(c, gm)

    @pl.when(even)
    def _():
        greet(c, gp2)
        greet(c, gm2)

    @pl.when(c > 0)
    def _():
        greet(c - 1, g)

    @pl.when(c < N_CUTS - 1)
    def _():
        greet(c + 1, g)

    @pl.when(c == 4)
    def _():
        greet(6, g)
        greet(7, g)

    @pl.when(c >= 6)
    def _():
        greet(4, g)
        greet(3, g)

    @pl.when(c == 3)
    def _():
        greet(6, g)
        greet(7, g)

    pl.when(c == 5)(lambda: greet(2, g))
    pl.when(c == 2)(lambda: greet(5, g))

    greet(c, g + 2 - 4 * lax.rem(g // 2, 2))
    for n in range(1, 8):
        greet(c, lax.rem(g + 4 * n, N_GZ))

    vt[:, pl.ds(0, 2)] = jnp.zeros((7, 2, K, LY), F32)
    vt[:, pl.ds(LX + 2, 2)] = jnp.zeros((7, 2, K, LY), F32)
    for edge in (fs, gs):
        edge[0, :, 7] = jnp.zeros((3, K, LY), F32)
        edge[NC + 1, :, 0] = jnp.zeros((3, K, LY), F32)
    ons[:, pl.ds(0, 8)] = jnp.zeros((5, 8, LY), F32)
    ons[:, pl.ds(8 + LX, 8)] = jnp.zeros((5, 8, LY), F32)
    acc[...] = jnp.zeros_like(acc)

    @pl.when(c == N_CUTS - 1)
    def _():
        @pl.loop(0, LX)
        def _(x):
            for z in range(3):
                gs[1 + x // XR, z, lax.rem(x, XR)] = jnp.zeros((K, LY), F32)

    def one(p):
        return jnp.where(p, 1, 0)

    partners = 10 + 2 * one(even) + one(c > 0) + one(c < N_CUTS - 1) + one(c == 5) + one(c == 2)
    pl.semaphore_wait(barrier, partners + 2 * (one(c >= 6) + one(c == 4) + one(c == 3)))

    on_up = remote(on_hbm, ons.at[pl.ds(0, 2), pl.ds(8, LX)], on_s.at[1], on_r.at[0], c, gp)
    on_dn = remote(on_hbm.at[pl.ds(0, 1)], ons.at[pl.ds(4, 1), pl.ds(8, LX)], on_s.at[2], on_r.at[1], c, gm)
    on_up.start()
    on_dn.start()

    def v_send(i):
        own(i, 0).wait()
        own(i, 1).wait()
        up(i).start()
        down(i).start()
        pl.when(even)(lambda: far(i).start())

    pl.loop(0, AHEAD)(v_send)

    ctr, ih, c0, c1, c2 = ctr_ref[0], ih_ref[0], cheb[0, 0], cheb[0, 1], cheb[0, 2]

    def arrive(i):
        up(i).wait_recv()
        pl.when(even)(lambda: forward(i).start())
        down(i).wait_recv()
        far(i).wait_recv()
        to = pl.ds(2 + i * XR, XR)
        vt[0, to] = jnp.swapaxes(far_in[i], 0, 1)

        @pl.loop(0, 2)
        def _(z):
            vt[1 + z, to] = jnp.swapaxes(below[i, z], 0, 1)
            vt[3 + z, to] = jnp.swapaxes(mine[i, z], 0, 1)
            vt[5 + z, to] = jnp.swapaxes(above[i, z], 0, 1)

    def apply_filter(i):
        @pl.loop(0, XR + 2)
        def _(r):
            x = i * XR - 1 + r
            for z in range(1, 6):
                v = vt[z, 2 + x]
                d = jnp.broadcast_to(ons[z - 1, pl.ds(8 + x, 1), :], (K, LY))
                around = vt[z - 1, 2 + x] + vt[z + 1, 2 + x] + vt[z, 1 + x] + vt[z, 3 + x] + lanes(v)
                first[z - 1, r] = ih * ((d - ctr) * v - around)

        @pl.when(i == 0)
        def _():
            first[:, pl.ds(0, 1)] = jnp.zeros((5, 1, K, LY), F32)

        @pl.when(i == NC - 1)
        def _():
            first[:, pl.ds(XR + 1, 1)] = jnp.zeros((5, 1, K, LY), F32)

        @pl.loop(0, XR)
        def _(r):
            x = i * XR + r
            for z in range(3):
                v = vt[z + 2, 2 + x]
                f = first[z + 1, r + 1]
                d = jnp.broadcast_to(ons[z + 1, pl.ds(8 + x, 1), :], (K, LY))
                around = first[z, r + 1] + first[z + 2, r + 1] + first[z + 1, r] + first[z + 1, r + 2] + lanes(f)
                second = 2.0 * (ih * ((d - ctr) * f - around)) - v
                fs[1 + i, z, r] = c0 * v + c1 * f + c2 * second

    def send(i):
        row = row_of(i)
        pl.when((c > 0) & (c != 4))(lambda: by_core(lambda lo, n: y_direct(i, lo, n, c - 1).start()))
        pl.when((c == 4) & (row == 0))(lambda: by_core(lambda lo, n: y_direct(i, lo, n, 3).start()))
        pl.when((c == 4) & (row != 0))(lambda: by_core(lambda lo, n: y_relay(i, lo, n, 4 + row).start()))

    def pass_on(i, onward, here):
        @pl.when(here)
        def _():
            def act(lo, n):
                y_relay(i, lo, n, c).wait_recv()
                onward(i, lo, n).start()

            by_core(act)

    def pass_ons(i):
        row = row_of(i)
        pass_on(i, relay_on, (row >= 2) & (c == 4 + row))
        pass_on(i, relay_twice, (row == 1) & (c == 5))

    def pass_last(i):
        pass_on(i, relay_on, (row_of(i) == 1) & (c == 2))

    def g_arrive(i):
        @pl.when(c < N_CUTS - 1)
        def _():
            by_core(lambda lo, n: y_direct(i, lo, n, c).wait_recv())
            pl.when(even)(lambda: g_forward(i).start())
            pl.when(odd)(lambda: g_forward(i).wait_recv())

    def project(i):
        @pl.loop(0, XR)
        def _(r):
            x = i * XR + r
            before, after = x + XR - 1, x + XR + 1
            for z in range(2):
                at = pl.ds(pl.multiple_of((z * XR + r) * LY, LY), LY)
                d = jnp.broadcast_to(ons[z + 2, pl.ds(8 + x, 1), :], (K, LY))
                for part, field in enumerate((fs, gs)):
                    mid = field[1 + i, z + 1, r]
                    around = field[before // XR, z + 1, lax.rem(before, XR)] + field[after // XR, z + 1, lax.rem(after, XR)]
                    w = d * mid - (around + lanes(mid))
                    if z == 0:
                        w = w - 2.0 * (field[1 + i, 0, r] + field[1 + i, 2, r])
                    hi = mid.astype(BF16)
                    w_hi = w.astype(BF16)
                    ops[pl.ds(part * K, K), at] = hi
                    ops[pl.ds(64 + part * K, K), at] = (mid - hi.astype(F32)).astype(BF16)
                    ops[pl.ds(128 + part * K, K), at] = w_hi
                    ops[pl.ds(192 + part * K, K), at] = (w - w_hi.astype(F32)).astype(BF16)

        acc[...] += lax.dot_general(
            ops[pl.ds(0, 128)], ops[...], (((1,), (1,)), ((), ())), preferred_element_type=F32
        )
        out_f(i).start()
        out_g(i).start()

    own_on.wait()
    on_up.wait()
    on_dn.wait()
    arrive(0)

    lag = jnp.where(c == 3, LAG_FAR, LAG)

    @pl.loop(0, NC + LAG_FAR + 1)
    def _(i):
        @pl.when(i + 1 < NC)
        def _():
            arrive(i + 1)
            pl.when(i + AHEAD < NC)(lambda: v_send(i + AHEAD))

        @pl.when(i < NC - 1)
        def _():
            @pl.loop(i, jnp.where(i == NC - 2, NC, i + 1))
            def _(j):
                apply_filter(j)
                send(j)

        @pl.when((i >= 1) & (i <= NC))
        def _():
            pass_ons(i - 1)

        @pl.when((i >= 2) & (i <= NC + 1))
        def _():
            pass_last(i - 2)

        @pl.when((i >= lag) & (i < NC + lag))
        def _():
            g_arrive(i - lag)

        @pl.when((i >= lag + 1) & (i < NC + lag + 1))
        def _():
            project(i - lag - 1)

    a = acc[...]
    part[:, pl.ds(0, 64)] = (a[0:64, 0:64] + a[64:128, 64:128]) + (a[0:64, 64:128] + a[64:128, 0:64])
    part[:, pl.ds(64, 64)] = (a[0:64, 128:192] + a[64:128, 192:256]) + (a[0:64, 192:256] + a[64:128, 128:192])
    solve(c, g, remote, part, linv_ref, proj_ref, *solve_scratch)

    @pl.loop(0, NC)
    def _(i):
        up(i).wait_send()
        down(i).wait_send()

        @pl.when(even)
        def _():
            far(i).wait_send()
            forward(i).wait_send()
            pl.when(c < N_CUTS - 1)(lambda: g_forward(i).wait_send())

        pl.when(c > 0)(lambda: by_core(lambda lo, n: y_direct(i, lo, n, c).wait_send()))
        row = row_of(i)
        passed = (row >= 1) & ((c == 4 + row) | ((c == 2) & (row == 1)))
        pl.when(passed)(lambda: by_core(lambda lo, n: relay_on(i, lo, n).wait_send()))
        out_f(i).wait()
        out_g(i).wait()


def run_filter(v, onsite, center, inv_half, cheb):
    dma = pltpu.SemaphoreType.DMA
    anyspace = pl.BlockSpec(memory_space=pl.ANY)
    return pl.pallas_call(
        filter_kernel,
        out_shape=(
            jax.ShapeDtypeStruct((NC, 2, XR, K, LY), F32),
            jax.ShapeDtypeStruct((NC, 2, XR, K, LY), F32),
            jax.ShapeDtypeStruct((64, 64), F32),
            jax.ShapeDtypeStruct((1, 64, 64), F32),
        ),
        in_specs=[anyspace, anyspace] + [pl.BlockSpec(memory_space=pltpu.SMEM)] * 3,
        out_specs=(anyspace, anyspace, pl.BlockSpec(memory_space=pltpu.VMEM), pl.BlockSpec(memory_space=pltpu.VMEM)),
        scratch_shapes=[
            pltpu.VMEM((NC, 2, K, XR, LY), F32),
            pltpu.VMEM((NC, 2, K, XR, LY), F32),
            pltpu.VMEM((NC, 2, K, XR, LY), F32),
            pltpu.VMEM((NC, K, XR, LY), F32),
            pltpu.VMEM((7, LX + 4, K, LY), F32),
            pltpu.VMEM((5, XR + 2, K, LY), F32),
            pltpu.VMEM((NC + 2, 3, XR, K, LY), F32),
            pltpu.VMEM((NC + 2, 3, XR, K, LY), F32),
            pltpu.VMEM((256, 2 * XR * LY), BF16),
            pltpu.VMEM((128, 256), F32),
            pltpu.VMEM((5, LX + 16, LY), F32),
            pltpu.VMEM((NC // 4, 3, XR, K, LY), F32),
            dma((2, NC)), dma((3,)), dma((2,)),
            dma((NC,)), dma((NC,)), dma((NC,)), dma((NC,)), dma((NC,)), dma((NC,)), dma((NC,)),
            dma((NC,)), dma((NC,)), dma((NC // 4,)), dma((NC // 4,)), dma((NC,)), dma((NC,)), dma((2, NC)),
            pltpu.VMEM((64, 128), F32),
            pltpu.VMEM((2, 32, 128), F32), pltpu.VMEM((2, 32, 128), F32), pltpu.VMEM((8, 32, 128), F32),
            pltpu.VMEM((64, 128), F32),
            dma, dma, dma, dma, dma((7,)), dma((7,)), dma, dma,
        ],
        compiler_params=pltpu.CompilerParams(
            collective_id=0, has_side_effects=True, vmem_limit_bytes=60 << 20
        ),
        name="filter",
    )(v, onsite, center, inv_half, cheb)


def basis_kernel(linv_ref, p_ref, f_ref, g_ref, out_ref, proj_ref, tmp):
    proj_ref[...] = p_ref[...]
    linv = linv_ref[...]
    hi = linv.astype(BF16)
    lo = (linv - hi.astype(F32)).astype(BF16)
    left = jnp.concatenate([hi, lo, hi], 1)
    for n in range(4):
        for z in range(2):
            for x in range(0, XR, 2):
                right = []
                for s in range(2):
                    t = jnp.concatenate([f_ref[n, z, x + s], g_ref[n, z, x + s]], 0)
                    t_hi = t.astype(BF16)
                    t_lo = (t - t_hi.astype(F32)).astype(BF16)
                    right.append(jnp.concatenate([t_hi, t_hi, t_lo], 0))
                got = jnp.dot(left, jnp.concatenate(right, 1), preferred_element_type=F32)
                tmp[x] = got[:, :LY]
                tmp[x + 1] = got[:, LY:]
            out_ref[0, :, z, pl.ds(n * XR, XR)] = jnp.swapaxes(tmp[...], 0, 1)


def run_basis(linv, p, f, g):
    small = pl.BlockSpec((1, 64, 64), lambda i: (0, 0, 0))
    half = pl.BlockSpec((4, 2, XR, K, LY), lambda i: (i, 0, 0, 0, 0))
    return pl.pallas_call(
        basis_kernel,
        out_shape=(jax.ShapeDtypeStruct((1, 2 * K, 2, LX, LY), F32), jax.ShapeDtypeStruct((1, 64, 64), F32)),
        grid=(NC // 4,),
        in_specs=[pl.BlockSpec((64, 64), lambda i: (0, 0)), small, half, half],
        out_specs=(pl.BlockSpec((1, 2 * K, 2, 4 * XR, LY), lambda i: (0, 0, 0, i, 0)), small),
        scratch_shapes=[pltpu.VMEM((XR, 2 * K, LY), F32)],
        compiler_params=pltpu.CompilerParams(vmem_limit_bytes=60 << 20),
        name="basis",
    )(linv, p, f, g)


def body(vectors, onsite, center, inv_half, cheb_coef):
    f, g, linv, projected = run_filter(vectors[0], onsite, center, inv_half, cheb_coef)
    return run_basis(linv, projected, f, g)


def solution(mesh):
    in_specs = (
        P("cuts", None, "gz", None, None),
        P("gz", None, None),
        P("cuts"),
        P("cuts"),
        P("cuts", None),
    )
    out_specs = (P("cuts", None, "gz", None, None), P("cuts", None, None))
    return jax.shard_map(body, mesh=mesh, in_specs=in_specs, out_specs=out_specs, check_vma=False)
```

```python
import functools

import jax
import jax.numpy as jnp
from jax import lax
from jax.experimental import pallas as pl
from jax.experimental.pallas import tpu as pltpu
from jax.sharding import PartitionSpec as P

MESH = pl.DeviceIdType.MESH
K = 32
LX = 128
LY = 128
XR = 8
NC = LX // XR
LAG = 2
LAG_FAR = 5
AHEAD = 3
N_CUTS = 8
N_GZ = 32
SITES = 64 * 128 * 128
F32 = jnp.float32
BF16 = jnp.bfloat16


def lanes(v):
    at = lax.broadcasted_iota(jnp.int32, v.shape, v.ndim - 1)
    left = jnp.where(at == 0, 0.0, pltpu.roll(v, 1, v.ndim - 1))
    right = jnp.where(at == LY - 1, 0.0, pltpu.roll(v, LY - 1, v.ndim - 1))
    return left + right


def solve(c, g, remote, part, linv_ref, proj_ref, half, got, zbuf, full, core_s, core_r, x_s, x_r, z_s, z_r, b_s, b_r):
    k = lax.rem(g, 2)
    z = g // 4
    mate = g + 1 - 2 * k
    across = g + 2 - 4 * lax.rem(g // 2, 2)
    peers = [lax.rem(g + 4 * n, N_GZ) for n in range(1, 8)]

    my_rows = pl.ds(pl.multiple_of(32 * k, 32), 32)
    theirs = pl.ds(pl.multiple_of(32 - 32 * k, 32), 32)
    step = remote(part.at[theirs], got.at[0], core_s, core_r, c, mate)
    step.start()
    step.wait()
    half[0] = part[my_rows] + got[0]
    step = remote(half.at[0], got.at[1], x_s, x_r, c, across)
    step.start()
    step.wait()
    total = half[0] + got[1]
    half[1] = total
    zbuf[z] = total
    sends = [remote(half.at[1], zbuf.at[z], z_s.at[n - 1], z_r.at[n - 1], c, peers[n - 1]) for n in range(1, 8)]
    for s in sends:
        s.start()
    for n in range(1, 8):
        remote(half.at[1], zbuf.at[lax.rem(z - n + 8, 8)], z_s.at[n - 1], z_r.at[n - 1], c, peers[n - 1]).wait_recv()
    for s in sends:
        s.wait_send()
    t = [zbuf[n] for n in range(8)]
    full[my_rows] = ((t[0] + t[1]) + (t[2] + t[3])) + ((t[4] + t[5]) + (t[6] + t[7]))
    step = remote(full.at[my_rows], full.at[my_rows], b_s, b_r, c, mate)
    step.start()
    remote(full.at[theirs], full.at[theirs], b_s, b_r, c, mate).wait_recv()
    step.wait_send()

    both = full[...] * (1.0 / SITES)
    sub = lax.broadcasted_iota(jnp.int32, (64, 128), 0)
    lane = lax.broadcasted_iota(jnp.int32, (64, 128), 1)
    m = both[:, 64:128]
    a = jnp.where(lane < 64, both, 0.0) + jnp.where(lane == sub, 0.25, 0.0) + jnp.where(lane == sub + 64, 1.0, 0.0)
    for i in range(63):
        row = a[i : i + 1, :]
        scaled = row / row[:, i : i + 1]
        lo = (i + 1) // 8 * 8
        low = a[lo:, :]
        col = jnp.where(sub[lo:, :] > i, jnp.broadcast_to(low[:, i : i + 1], low.shape), 0.0)
        low = low - col * scaled
        a = low if lo == 0 else jnp.concatenate([a[:lo, :], low], 0)
    diag = jnp.sum(jnp.where(lane == sub, a, 0.0), axis=1, keepdims=True)
    linv = a[:, 64:128] * (1.0 / jnp.sqrt(diag))
    linv_ref[...] = linv

    def exact(p, q, dims):
        return lax.dot_general(p, q, (dims, ((), ())), precision=lax.Precision.HIGHEST, preferred_element_type=F32)

    right = exact(m, linv, ((1,), (1,)))
    p = exact(linv, right, ((1,), (0,)))
    proj_ref[0] = 0.5 * (p + p.T)


def filter_kernel(
    v_hbm, on_hbm, ctr_ref, ih_ref, cheb, f_hbm, g_hbm, linv_ref, proj_ref,
    mine, below, above, far_in, vt, first, fs, gs, ops, acc, ons, relay,
    own_s, on_s, on_r, up_s, up_r, dn_s, dn_r, far_s, far_r, fwd_s, y_s, y_r,
    rel_s, rel_r, gf_s, gf_r, out_s, part, *solve_scratch,
):
    c = lax.axis_index("cuts")
    g = lax.axis_index("gz")
    k = lax.rem(g, 2)
    even, odd = k == 0, k == 1
    gp = lax.rem(g + 1, N_GZ)
    gm = lax.rem(g + N_GZ - 1, N_GZ)
    gp2 = lax.rem(g + 2, N_GZ)
    gm2 = lax.rem(g + N_GZ - 2, N_GZ)

    def remote(src, dst, ss, rs, cc, gg):
        return pltpu.make_async_remote_copy(
            src_ref=src, dst_ref=dst, send_sem=ss, recv_sem=rs, device_id=(cc, gg), device_id_type=MESH
        )

    def rows(i):
        return pl.ds(pl.multiple_of(i * XR, XR), XR)

    def own(i, z):
        return pltpu.make_async_copy(v_hbm.at[:, z, rows(i)], mine.at[i, z], own_s.at[z, i])

    def up(i):
        return remote(mine.at[i], below.at[i], up_s.at[i], up_r.at[i], c, gp)

    def down(i):
        return remote(mine.at[i], above.at[i], dn_s.at[i], dn_r.at[i], c, gm)

    def far(i):
        return remote(mine.at[i, 1], far_in.at[i], far_s.at[i], far_r.at[i], c, gp2)

    def forward(i):
        return remote(below.at[i, 1], far_in.at[i], fwd_s.at[i], far_r.at[i], c, gp)

    def y_direct(i, lo, n, cc):
        return remote(fs.at[1 + i, pl.ds(lo, n)], gs.at[1 + i, pl.ds(lo, n)], y_s.at[i], y_r.at[i], cc, g)

    def y_relay(i, lo, n, cc):
        return remote(fs.at[1 + i, pl.ds(lo, n)], relay.at[i // 4, pl.ds(lo, n)], y_s.at[i], rel_r.at[i // 4], cc, g)

    def relay_on(i, lo, n):
        return remote(relay.at[i // 4, pl.ds(lo, n)], gs.at[1 + i, pl.ds(lo, n)], rel_s.at[i // 4], y_r.at[i], 3, g)

    def relay_twice(i, lo, n):
        return remote(
            relay.at[i // 4, pl.ds(lo, n)], relay.at[i // 4, pl.ds(lo, n)], rel_s.at[i // 4], rel_r.at[i // 4], 2, g
        )

    def g_forward(i):
        return remote(gs.at[1 + i, 2], gs.at[1 + i, 0], gf_s.at[i], gf_r.at[i], c, gp)

    def out_f(i):
        return pltpu.make_async_copy(fs.at[1 + i, pl.ds(1, 2)], f_hbm.at[i], out_s.at[0, i])

    def out_g(i):
        return pltpu.make_async_copy(gs.at[1 + i, pl.ds(1, 2)], g_hbm.at[i], out_s.at[1, i])

    def row_of(i):
        m = lax.rem(i, 4)
        return jnp.where(m == 0, 1, jnp.where(m == 1, 3, jnp.where(m == 2, 2, 0)))

    def row_of(i):
        m = lax.rem(i, 4)
        return jnp.where(m == 0, 1, jnp.where(m == 1, 3, jnp.where(m == 2, 2, 0)))

    def by_core(act):
        pl.when(even)(lambda: act(0, 3))
        pl.when(odd)(lambda: act(1, 2))

    @pl.loop(0, NC)
    def _(i):
        own(i, 0).start()
        own(i, 1).start()

    own_on = pltpu.make_async_copy(on_hbm, ons.at[pl.ds(2, 2), pl.ds(8, LX)], on_s.at[0])
    own_on.start()

    barrier = pltpu.get_barrier_semaphore()

    def greet(cc, gg):
        pl.semaphore_signal(barrier, inc=1, device_id=(cc, gg), device_id_type=MESH)

    greet(c, gp)
    greet(c, gm)

    @pl.when(even)
    def _():
        greet(c, gp2)
        greet(c, gm2)

    @pl.when(c > 0)
    def _():
        greet(c - 1, g)

    @pl.when(c < N_CUTS - 1)
    def _():
        greet(c + 1, g)

    @pl.when(c == 4)
    def _():
        greet(6, g)
        greet(7, g)

    @pl.when(c >= 6)
    def _():
        greet(4, g)
        greet(3, g)

    @pl.when(c == 3)
    def _():
        greet(6, g)
        greet(7, g)

    pl.when(c == 5)(lambda: greet(2, g))
    pl.when(c == 2)(lambda: greet(5, g))

    greet(c, g + 2 - 4 * lax.rem(g // 2, 2))
    for n in range(1, 8):
        greet(c, lax.rem(g + 4 * n, N_GZ))

    vt[:, pl.ds(0, 2)] = jnp.zeros((7, 2, K, LY), F32)
    vt[:, pl.ds(LX + 2, 2)] = jnp.zeros((7, 2, K, LY), F32)
    for edge in (fs, gs):
        edge[0, :, 7] = jnp.zeros((3, K, LY), F32)
        edge[NC + 1, :, 0] = jnp.zeros((3, K, LY), F32)
    ons[:, pl.ds(0, 8)] = jnp.zeros((5, 8, LY), F32)
    ons[:, pl.ds(8 + LX, 8)] = jnp.zeros((5, 8, LY), F32)
    acc[...] = jnp.zeros_like(acc)

    @pl.when(c == N_CUTS - 1)
    def _():
        @pl.loop(0, LX)
        def _(x):
            for z in range(3):
                gs[1 + x // XR, z, lax.rem(x, XR)] = jnp.zeros((K, LY), F32)

    def one(p):
        return jnp.where(p, 1, 0)

    partners = 10 + 2 * one(even) + one(c > 0) + one(c < N_CUTS - 1) + one(c == 5) + one(c == 2)
    pl.semaphore_wait(barrier, partners + 2 * (one(c >= 6) + one(c == 4) + one(c == 3)))

    on_up = remote(on_hbm, ons.at[pl.ds(0, 2), pl.ds(8, LX)], on_s.at[1], on_r.at[0], c, gp)
    on_dn = remote(on_hbm.at[pl.ds(0, 1)], ons.at[pl.ds(4, 1), pl.ds(8, LX)], on_s.at[2], on_r.at[1], c, gm)
    on_up.start()
    on_dn.start()

    def v_send(i):
        own(i, 0).wait()
        own(i, 1).wait()
        up(i).start()
        down(i).start()
        pl.when(even)(lambda: far(i).start())

    pl.loop(0, AHEAD)(v_send)

    ctr, ih, c0, c1, c2 = ctr_ref[0], ih_ref[0], cheb[0, 0], cheb[0, 1], cheb[0, 2]

    def arrive(i):
        up(i).wait_recv()
        pl.when(even)(lambda: forward(i).start())
        down(i).wait_recv()
        far(i).wait_recv()
        to = pl.ds(2 + i * XR, XR)
        vt[0, to] = jnp.swapaxes(far_in[i], 0, 1)

        @pl.loop(0, 2)
        def _(z):
            vt[1 + z, to] = jnp.swapaxes(below[i, z], 0, 1)
            vt[3 + z, to] = jnp.swapaxes(mine[i, z], 0, 1)
            vt[5 + z, to] = jnp.swapaxes(above[i, z], 0, 1)

    def apply_filter(i):
        @pl.loop(0, XR + 2)
        def _(r):
            x = i * XR - 1 + r
            for z in range(1, 6):
                v = vt[z, 2 + x]
                d = jnp.broadcast_to(ons[z - 1, pl.ds(8 + x, 1), :], (K, LY))
                around = vt[z - 1, 2 + x] + vt[z + 1, 2 + x] + vt[z, 1 + x] + vt[z, 3 + x] + lanes(v)
                first[z - 1, r] = ih * ((d - ctr) * v - around)

        @pl.when(i == 0)
        def _():
            first[:, pl.ds(0, 1)] = jnp.zeros((5, 1, K, LY), F32)

        @pl.when(i == NC - 1)
        def _():
            first[:, pl.ds(XR + 1, 1)] = jnp.zeros((5, 1, K, LY), F32)

        @pl.loop(0, XR)
        def _(r):
            x = i * XR + r
            for z in range(3):
                v = vt[z + 2, 2 + x]
                f = first[z + 1, r + 1]
                d = jnp.broadcast_to(ons[z + 1, pl.ds(8 + x, 1), :], (K, LY))
                around = first[z, r + 1] + first[z + 2, r + 1] + first[z + 1, r] + first[z + 1, r + 2] + lanes(f)
                second = 2.0 * (ih * ((d - ctr) * f - around)) - v
                fs[1 + i, z, r] = c0 * v + c1 * f + c2 * second

    def send(i):
        row = row_of(i)
        pl.when((c > 0) & (c != 4))(lambda: by_core(lambda lo, n: y_direct(i, lo, n, c - 1).start()))
        pl.when((c == 4) & (row == 0))(lambda: by_core(lambda lo, n: y_direct(i, lo, n, 3).start()))
        pl.when((c == 4) & (row != 0))(lambda: by_core(lambda lo, n: y_relay(i, lo, n, 4 + row).start()))

    def pass_on(i, onward, here):
        @pl.when(here)
        def _():
            def act(lo, n):
                y_relay(i, lo, n, c).wait_recv()
                onward(i, lo, n).start()

            by_core(act)

    def pass_ons(i):
        row = row_of(i)
        pass_on(i, relay_on, (row >= 2) & (c == 4 + row))
        pass_on(i, relay_twice, (row == 1) & (c == 5))

    def pass_last(i):
        pass_on(i, relay_on, (row_of(i) == 1) & (c == 2))

    def g_arrive(i):
        @pl.when(c < N_CUTS - 1)
        def _():
            by_core(lambda lo, n: y_direct(i, lo, n, c).wait_recv())
            pl.when(even)(lambda: g_forward(i).start())
            pl.when(odd)(lambda: g_forward(i).wait_recv())

    def project(i):
        @pl.loop(0, XR)
        def _(r):
            x = i * XR + r
            before, after = x + XR - 1, x + XR + 1
            for z in range(2):
                at = pl.ds(pl.multiple_of((z * XR + r) * LY, LY), LY)
                d = jnp.broadcast_to(ons[z + 2, pl.ds(8 + x, 1), :], (K, LY))
                for part, field in enumerate((fs, gs)):
                    mid = field[1 + i, z + 1, r]
                    around = field[before // XR, z + 1, lax.rem(before, XR)] + field[after // XR, z + 1, lax.rem(after, XR)]
                    w = d * mid - (around + lanes(mid))
                    if z == 0:
                        w = w - 2.0 * (field[1 + i, 0, r] + field[1 + i, 2, r])
                    hi = mid.astype(BF16)
                    w_hi = w.astype(BF16)
                    ops[pl.ds(part * K, K), at] = hi
                    ops[pl.ds(64 + part * K, K), at] = (mid - hi.astype(F32)).astype(BF16)
                    ops[pl.ds(128 + part * K, K), at] = w_hi
                    ops[pl.ds(192 + part * K, K), at] = (w - w_hi.astype(F32)).astype(BF16)

        acc[...] += lax.dot_general(
            ops[pl.ds(0, 128)], ops[...], (((1,), (1,)), ((), ())), preferred_element_type=F32
        )
        out_f(i).start()
        out_g(i).start()

    own_on.wait()
    on_up.wait()
    on_dn.wait()
    arrive(0)

    lag = jnp.where(c == 3, LAG_FAR, LAG)

    @pl.loop(0, NC + LAG_FAR + 1)
    def _(i):
        @pl.when(i + 1 < NC)
        def _():
            arrive(i + 1)
            pl.when(i + AHEAD < NC)(lambda: v_send(i + AHEAD))

        @pl.when(i < NC - 1)
        def _():
            @pl.loop(i, jnp.where(i == NC - 2, NC, i + 1))
            def _(j):
                apply_filter(j)
                send(j)

        @pl.when((i >= 1) & (i <= NC))
        def _():
            pass_ons(i - 1)

        @pl.when((i >= 2) & (i <= NC + 1))
        def _():
            pass_last(i - 2)

        @pl.when((i >= lag) & (i < NC + lag))
        def _():
            g_arrive(i - lag)

        @pl.when((i >= lag + 1) & (i < NC + lag + 1))
        def _():
            project(i - lag - 1)

    a = acc[...]
    part[:, pl.ds(0, 64)] = (a[0:64, 0:64] + a[64:128, 64:128]) + (a[0:64, 64:128] + a[64:128, 0:64])
    part[:, pl.ds(64, 64)] = (a[0:64, 128:192] + a[64:128, 192:256]) + (a[0:64, 192:256] + a[64:128, 128:192])
    solve(c, g, remote, part, linv_ref, proj_ref, *solve_scratch)

    @pl.loop(0, NC)
    def _(i):
        up(i).wait_send()
        down(i).wait_send()

        @pl.when(even)
        def _():
            far(i).wait_send()
            forward(i).wait_send()
            pl.when(c < N_CUTS - 1)(lambda: g_forward(i).wait_send())

        pl.when(c > 0)(lambda: by_core(lambda lo, n: y_direct(i, lo, n, c).wait_send()))
        row = row_of(i)
        passed = (row >= 1) & ((c == 4 + row) | ((c == 2) & (row == 1)))
        pl.when(passed)(lambda: by_core(lambda lo, n: relay_on(i, lo, n).wait_send()))
        out_f(i).wait()
        out_g(i).wait()


def run_filter(v, onsite, center, inv_half, cheb):
    dma = pltpu.SemaphoreType.DMA
    anyspace = pl.BlockSpec(memory_space=pl.ANY)
    return pl.pallas_call(
        filter_kernel,
        out_shape=(
            jax.ShapeDtypeStruct((NC, 2, XR, K, LY), F32),
            jax.ShapeDtypeStruct((NC, 2, XR, K, LY), F32),
            jax.ShapeDtypeStruct((64, 64), F32),
            jax.ShapeDtypeStruct((1, 64, 64), F32),
        ),
        in_specs=[anyspace, anyspace] + [pl.BlockSpec(memory_space=pltpu.SMEM)] * 3,
        out_specs=(anyspace, anyspace, pl.BlockSpec(memory_space=pltpu.VMEM), pl.BlockSpec(memory_space=pltpu.VMEM)),
        scratch_shapes=[
            pltpu.VMEM((NC, 2, K, XR, LY), F32),
            pltpu.VMEM((NC, 2, K, XR, LY), F32),
            pltpu.VMEM((NC, 2, K, XR, LY), F32),
            pltpu.VMEM((NC, K, XR, LY), F32),
            pltpu.VMEM((7, LX + 4, K, LY), F32),
            pltpu.VMEM((5, XR + 2, K, LY), F32),
            pltpu.VMEM((NC + 2, 3, XR, K, LY), F32),
            pltpu.VMEM((NC + 2, 3, XR, K, LY), F32),
            pltpu.VMEM((256, 2 * XR * LY), BF16),
            pltpu.VMEM((128, 256), F32),
            pltpu.VMEM((5, LX + 16, LY), F32),
            pltpu.VMEM((NC // 4, 3, XR, K, LY), F32),
            dma((2, NC)), dma((3,)), dma((2,)),
            dma((NC,)), dma((NC,)), dma((NC,)), dma((NC,)), dma((NC,)), dma((NC,)), dma((NC,)),
            dma((NC,)), dma((NC,)), dma((NC // 4,)), dma((NC // 4,)), dma((NC,)), dma((NC,)), dma((2, NC)),
            pltpu.VMEM((64, 128), F32),
            pltpu.VMEM((2, 32, 128), F32), pltpu.VMEM((2, 32, 128), F32), pltpu.VMEM((8, 32, 128), F32),
            pltpu.VMEM((64, 128), F32),
            dma, dma, dma, dma, dma((7,)), dma((7,)), dma, dma,
        ],
        compiler_params=pltpu.CompilerParams(
            collective_id=0, has_side_effects=True, vmem_limit_bytes=60 << 20
        ),
        name="filter",
    )(v, onsite, center, inv_half, cheb)


def basis_kernel(linv_ref, p_ref, f_ref, g_ref, out_ref, proj_ref, tmp):
    proj_ref[...] = p_ref[...]
    linv = linv_ref[...]
    hi = linv.astype(BF16)
    lo = (linv - hi.astype(F32)).astype(BF16)
    left = jnp.concatenate([hi, lo, hi], 1)
    for n in range(8):
        for z in range(2):
            for x in range(0, XR, 2):
                right = []
                for s in range(2):
                    t = jnp.concatenate([f_ref[n, z, x + s], g_ref[n, z, x + s]], 0)
                    t_hi = t.astype(BF16)
                    t_lo = (t - t_hi.astype(F32)).astype(BF16)
                    right.append(jnp.concatenate([t_hi, t_hi, t_lo], 0))
                got = jnp.dot(left, jnp.concatenate(right, 1), preferred_element_type=F32)
                tmp[x] = got[:, :LY]
                tmp[x + 1] = got[:, LY:]
            out_ref[0, :, z, pl.ds(n * XR, XR)] = jnp.swapaxes(tmp[...], 0, 1)


def run_basis(linv, p, f, g):
    small = pl.BlockSpec((1, 64, 64), lambda i: (0, 0, 0))
    half = pl.BlockSpec((8, 2, XR, K, LY), lambda i: (i, 0, 0, 0, 0))
    return pl.pallas_call(
        basis_kernel,
        out_shape=(jax.ShapeDtypeStruct((1, 2 * K, 2, LX, LY), F32), jax.ShapeDtypeStruct((1, 64, 64), F32)),
        grid=(NC // 8,),
        in_specs=[pl.BlockSpec((64, 64), lambda i: (0, 0)), small, half, half],
        out_specs=(pl.BlockSpec((1, 2 * K, 2, 8 * XR, LY), lambda i: (0, 0, 0, i, 0)), small),
        scratch_shapes=[pltpu.VMEM((XR, 2 * K, LY), F32)],
        compiler_params=pltpu.CompilerParams(vmem_limit_bytes=60 << 20),
        name="basis",
    )(linv, p, f, g)


def body(vectors, onsite, center, inv_half, cheb_coef):
    f, g, linv, projected = run_filter(vectors[0], onsite, center, inv_half, cheb_coef)
    return run_basis(linv, projected, f, g)


def solution(mesh):
    in_specs = (
        P("cuts", None, "gz", None, None),
        P("gz", None, None),
        P("cuts"),
        P("cuts"),
        P("cuts", None),
    )
    out_specs = (P("cuts", None, "gz", None, None), P("cuts", None, None))
    return jax.shard_map(body, mesh=mesh, in_specs=in_specs, out_specs=out_specs, check_vma=False)
```
